128 devices in a mesh: tile: 16 (over z_lo, x, core), mode: 8 (over y, z_hi).
Axes of the slice: x: 4, y: 4, z: 4 (z_hi: 2, z_lo: 2; z = z_hi * 2 + z_lo), core: 2. Of those that a mesh axis runs over, the one named last changes fastest.
Arguments:
- object_field: float32 [2, 2, 4096, 384], P(None, None, 'tile'), may hold values from -4 to 4
- probe: float32 [8, 2, 256, 256], P('mode'), may hold values from -4 to 4
- measured: float32 [64, 256, 256], P('tile'), may hold values from 0 to 16
- prop_phase: float32 [256, 256], replicated, may hold values from -3.140625 to 3.140625
- counts: int32 [16], P('tile'), may hold values from 1 to 4, 32 in all
- row_offset: int32 [64], P('tile'), may hold values from 0 to 255
- col_offset: int32 [64], P('tile'), may hold values from 0 to 128
Outputs:
- object_grad: float32 [2, 2, 4096, 384], P(None, None, 'tile')
- probe_grad: float32 [8, 2, 256, 256], P('mode')
The draws below stay inside these ranges and needn't reach their ends.
Inputs may be any that keep to these rules, and one draw needn't show every extreme that they name: Slot i is live for i % 4 < counts[i // 4]; some tile has all 4 slots live.
All inputs are finite; a program needn't handle non-finite values. No bound on the sum of `counts` on one device may be relied on, other than what follows from the above.
Results may differ from the reference program's by a relative error of at most 0.0003.
Values sent between devices are 32-bit elements; how exact they have to be, the bound alone decides.
No kernel may reach another device: no remote copies, remote signals or barrier semaphores. Data moves between devices by JAX's collectives and lax.ppermute only.
A program may use at most 128 MiB of HBM per device.

```python
import math
import jax
import jax.numpy as jnp
import numpy as np
from jax import lax

WIN = 256
MODES = 8
SLICES = 2
CAP = 4
TILE_ROWS = 256
COLS = 384
ROWS = 4096
POSITIONS = 64
N_TILE = 16


def with_ends(values, key, least, largest):
    shape = values.shape
    spot = [jax.random.randint(jax.random.fold_in(key, axis), (), 0, shape[axis]) for axis in range(len(shape))]
    values = values.at[tuple(spot)].set(least)
    longest = shape.index(max(shape))
    spot[longest] = (spot[longest] + 1) % shape[longest]
    return values.at[tuple(spot)].set(largest)


def block_scale(stream_key, extent, split, least, high):
    gain, own = 1.0, jax.random.fold_in(stream_key, 6)
    for dim, parts in split:
        heights = jnp.exp(jax.random.uniform(jax.random.fold_in(own, dim), (parts,), jnp.float32, least / len(split), high / len(split)))
        gain = gain * jnp.repeat(heights, extent[dim] // parts).reshape([-1 if axis == dim else 1 for axis in range(len(extent))])
    return gain


def split_up(number_of, total, limit, slope):
    portions = [(1 << 20) // math.isqrt(grade ** slope) + 1 for grade in range(2, number_of + 1)]
    rest, given = total - limit - (number_of - 1), [1] * (number_of - 1)
    while rest > 0:
        free = [i for i in range(number_of - 1) if given[i] < limit]
        mass, left = sum([portions[i] for i in free]), rest
        for i in free:
            extra = min(limit - given[i], max(1, left * portions[i] // mass), rest)
            given[i] = given[i] + extra
            rest = rest - extra
    return np.array([limit] + given)


def ragged_sizes(own_key, amount, total, most, lean):
    if amount == 2:
        one = jax.random.randint(own_key, (), max(1, total - most), min(most, total - 1) + 1)
        return jnp.stack([one, total - one])
    sizes = jnp.asarray(split_up(amount, total, most, lean), jnp.int32)
    pairs = (amount - 1) // 2
    giver, receiver = sizes[1:1 + 2 * pairs:2], sizes[2:2 + 2 * pairs:2]
    margin = jnp.minimum(giver - 1, most - receiver)
    moved = jax.random.randint(jax.random.fold_in(own_key, 1), (pairs,), 0, 1 << 20) % (margin + 1)
    sizes = sizes.at[1:1 + 2 * pairs:2].set(giver - moved).at[2:2 + 2 * pairs:2].set(receiver + moved)
    return sizes[jax.random.permutation(jax.random.fold_in(own_key, 2), amount)]


def scatter_about(own_key, shape, spread, most, shards=(), kind=jnp.bfloat16):
    drawn = jax.random.normal(own_key, shape, jnp.float32) * spread
    if len(shards) > 0:
        drawn = block_scale(own_key, shape, shards, -0.22, 0.18) * drawn
    return jnp.clip(drawn, min=-most, max=most).astype(kind)


def setup_inputs(seed: int = 0) -> dict:
    keys = jax.random.split(jax.random.key(seed), 8)
    return {
        "object_field": scatter_about(keys[0], (SLICES, 2, ROWS, COLS), 0.7, 4.0, ((2, 16),), jnp.float32),
        "probe": scatter_about(keys[1], (MODES, 2, WIN, WIN), 0.7, 4.0, ((0, 8),), jnp.float32),
        "measured": jnp.clip(16.0 * jax.random.uniform(keys[2], (POSITIONS, WIN, WIN), jnp.float32) ** block_scale(keys[2], (POSITIONS, WIN, WIN), ((0, 16),), -0.2, 0.2), 0.0, 16.0),
        "prop_phase": jnp.clip(jax.random.uniform(keys[3], (WIN, WIN), jnp.float32, -3.140625, 3.140625), -3.140625, 3.140625),
        "counts": ragged_sizes(keys[4], N_TILE, N_TILE * CAP // 2, CAP, 2).astype(jnp.int32),
        "row_offset": with_ends(jax.random.randint(keys[5], (POSITIONS,), 0, TILE_ROWS), jax.random.fold_in(keys[5], 1), 0, TILE_ROWS - 1).astype(jnp.int32),
        "col_offset": with_ends(jax.random.randint(keys[6], (POSITIONS,), 0, COLS - WIN + 1), jax.random.fold_in(keys[6], 1), 0, COLS - WIN).astype(jnp.int32),
    }


def forward_two(field):
    return jnp.fft.fft2(field, norm="ortho")


def inverse_two(field):
    return jnp.fft.ifft2(field, norm="ortho")


def reference(object_field, probe, measured, prop_phase, counts, row_offset, col_offset):
    layers = object_field.shape[0]
    padded = jnp.pad(object_field, ((0, 0), (0, 0), (0, WIN), (0, 0)))
    obj_wave = lax.complex(padded[:, 0], padded[:, 1])
    probe_wave = lax.complex(probe[:, 0], probe[:, 1])
    kernel = lax.complex(jnp.cos(prop_phase), jnp.sin(prop_phase))
    slot_ids = jnp.arange(N_TILE * CAP, dtype=jnp.int32)
    owners = slot_ids // CAP
    live = ((slot_ids % CAP) < counts[owners]).astype(object_field.dtype)
    rows_start = (owners * TILE_ROWS + row_offset).astype(jnp.int32)
    zero_index = jnp.zeros((), jnp.int32)

    def visit(carry, inputs):
        grad_obj, grad_probe = carry
        row_start, col_start, alive, target = inputs
        start = (zero_index, row_start.astype(jnp.int32), col_start.astype(jnp.int32))
        window = lax.dynamic_slice(obj_wave, start, (layers, WIN, WIN))
        wave = probe_wave * window[0]
        before = []
        for layer in range(1, layers):
            moved = inverse_two(kernel * forward_two(wave))
            before.append(moved)
            wave = moved * window[layer]
        far_field = forward_two(wave)
        intensity = jnp.sum(jnp.real(far_field) ** 2 + jnp.imag(far_field) ** 2, axis=0)
        weight = (intensity - target) / MODES * alive
        back = inverse_two(weight * far_field)
        pieces = [None] * layers
        for layer in range(layers - 1, 0, -1):
            pieces[layer] = jnp.sum(jnp.conj(before[layer - 1]) * back, axis=0)
            back = inverse_two(jnp.conj(kernel) * forward_two(jnp.conj(window[layer]) * back))
        pieces[0] = jnp.sum(jnp.conj(probe_wave) * back, axis=0)
        grad_probe = grad_probe + jnp.conj(window[0]) * back
        current = lax.dynamic_slice(grad_obj, start, (layers, WIN, WIN))
        grad_obj = lax.dynamic_update_slice(grad_obj, current + jnp.stack(pieces), start)
        return (grad_obj, grad_probe), None

    init = (jnp.zeros_like(obj_wave), jnp.zeros_like(probe_wave))
    (grad_obj, grad_probe), _ = lax.scan(visit, init, (rows_start, col_offset, live, measured))
    grad_obj = grad_obj[:, :N_TILE * TILE_ROWS]
    object_grad = jnp.stack([jnp.real(grad_obj), jnp.imag(grad_obj)], axis=1).astype(jnp.float32)
    probe_grad = jnp.stack([jnp.real(grad_probe), jnp.imag(grad_probe)], axis=1).astype(jnp.float32)
    return object_grad, probe_grad
```

```python
import math

import jax
import jax.numpy as jnp
import numpy as np
from jax import lax
from jax.experimental import pallas as pl
from jax.experimental.pallas import tpu as pltpu
from jax.sharding import Mesh, PartitionSpec as P


WIN = 256
HALF = 128
MODES = 8
COLS = 384
F32 = jnp.float32
BF16 = jnp.bfloat16
TILE = ("zl", "x", "core")
MODE = ("y", "zh")
SPREAD = ("zl", "x", "y")
VMEM = pl.BlockSpec(memory_space=pltpu.VMEM)
SMEM = pl.BlockSpec(memory_space=pltpu.SMEM)
PARAMS = pltpu.CompilerParams(vmem_limit_bytes=60 * 1024 * 1024)


def make_tables():
    index = np.arange(HALF)
    angle = (index[:, None] * index[None, :] % HALF) * (2.0 * math.pi / HALF)
    cosine, sine = np.cos(angle) / 16.0, np.sin(angle) / 16.0
    ahead = np.block([[cosine, -sine], [sine, cosine]])
    both = []
    for matrix in (ahead, ahead.T):
        high = matrix.astype(np.float32).astype(jnp.bfloat16)
        low = (matrix - high.astype(np.float64)).astype(np.float32).astype(jnp.bfloat16)
        both += [high, low]
    turn = index * (math.pi / HALF)
    lane = np.stack([np.cos(turn), np.sin(turn)])
    lane_table = np.broadcast_to(lane[:, None, :], (2, 8, HALF)).astype(np.float32)
    row_table = np.broadcast_to(lane[:, :, None], (2, HALF, HALF)).astype(np.float32)
    order = np.concatenate([np.arange(0, WIN, 2), np.arange(1, WIN, 2)])
    pick = np.zeros((WIN, WIN), np.float32)
    pick[np.arange(WIN), order] = 1.0
    picks = np.stack([pick, pick.T]).astype(jnp.bfloat16)
    return np.stack(both), lane_table, row_table, picks


def mm(left, right):
    return jnp.dot(left, right, preferred_element_type=F32)


def split(value):
    high = value.astype(BF16)
    return high, (value - high.astype(F32)).astype(BF16)


def dot_right(value, tables, which):
    high, low = split(value)
    return mm(high, tables[which]) + (mm(low, tables[which]) + mm(high, tables[which + 1]))


def dot_left(tables, which, value):
    high, low = split(value)
    return mm(tables[which], high) + (mm(tables[which], low) + mm(tables[which + 1], high))


def right_forward(real, imag, tables, lane):
    rows = real.shape[0]
    cosine, sine = lane[0, 0:1, :], lane[1, 0:1, :]
    ar, br, ai, bi = real[:, :HALF], real[:, HALF:], imag[:, :HALF], imag[:, HALF:]
    dr, di = ar - br, ai - bi
    top = jnp.concatenate([ar + br, ai + bi], axis=1)
    low = jnp.concatenate([dr * cosine + di * sine, di * cosine - dr * sine], axis=1)
    out = dot_right(jnp.concatenate([top, low], axis=0), tables, 0)
    even, odd = out[:rows], out[rows:]
    return (
        jnp.concatenate([even[:, :HALF], odd[:, :HALF]], axis=1),
        jnp.concatenate([even[:, HALF:], odd[:, HALF:]], axis=1),
    )


def right_inverse(real, imag, tables, lane):
    rows = real.shape[0]
    cosine, sine = lane[0, 0:1, :], lane[1, 0:1, :]
    even = jnp.concatenate([real[:, :HALF], imag[:, :HALF]], axis=1)
    odd = jnp.concatenate([real[:, HALF:], imag[:, HALF:]], axis=1)
    out = dot_right(jnp.concatenate([even, odd], axis=0), tables, 2)
    er, ei = out[:rows, :HALF], out[:rows, HALF:]
    pr, pi = out[rows:, :HALF], out[rows:, HALF:]
    tr, ti = pr * cosine - pi * sine, pi * cosine + pr * sine
    return (
        jnp.concatenate([er + tr, er - tr], axis=1),
        jnp.concatenate([ei + ti, ei - ti], axis=1),
    )


def left_forward(real, imag, tables, row):
    width = real.shape[1]
    cosine, sine = row[0], row[1]
    ar, br, ai, bi = real[:HALF], real[HALF:], imag[:HALF], imag[HALF:]
    dr, di = ar - br, ai - bi
    top = jnp.concatenate([ar + br, ai + bi], axis=0)
    low = jnp.concatenate([dr * cosine + di * sine, di * cosine - dr * sine], axis=0)
    out = dot_left(tables, 2, jnp.concatenate([top, low], axis=1))
    even, odd = out[:, :width], out[:, width:]
    return (
        jnp.concatenate([even[:HALF], odd[:HALF]], axis=0),
        jnp.concatenate([even[HALF:], odd[HALF:]], axis=0),
    )


def left_inverse(real, imag, tables, row):
    width = real.shape[1]
    cosine, sine = row[0], row[1]
    even = jnp.concatenate([real[:HALF], imag[:HALF]], axis=0)
    odd = jnp.concatenate([real[HALF:], imag[HALF:]], axis=0)
    out = dot_left(tables, 0, jnp.concatenate([even, odd], axis=1))
    er, ei = out[:HALF, :width], out[HALF:, :width]
    pr, pi = out[:HALF, width:], out[HALF:, width:]
    tr, ti = pr * cosine - pi * sine, pi * cosine + pr * sine
    return (
        jnp.concatenate([er + tr, er - tr], axis=0),
        jnp.concatenate([ei + ti, ei - ti], axis=0),
    )


def times(ar, ai, br, bi):
    return ar * br - ai * bi, ar * bi + ai * br


def times_conj(ar, ai, br, bi):
    return ar * br + ai * bi, ar * bi - ai * br


BLOCKS = (slice(0, HALF), slice(HALF, WIN))


def cut_window(own, halo, row, col, out):
    rows = lax.broadcasted_iota(jnp.int32, (WIN, COLS), 0)
    lanes = lax.broadcasted_iota(jnp.int32, (WIN, HALF), 1)
    for part in range(2):
        chosen = jnp.where(rows < row, halo[part], own[part])
        first = jnp.where(lanes < col, chosen[:, 2 * HALF :], chosen[:, :HALF])
        ring = jnp.concatenate([first, chosen[:, HALF : 2 * HALF]], axis=1)
        ring = pltpu.roll(ring, lax.rem(WIN - row, WIN), 0)
        out[part] = pltpu.roll(ring, lax.rem(WIN - col, WIN), 1)


def prepare_kernel(place, measured, wave, picks, kernel_out, measured_out):
    def reorder(value):
        for side in range(2):
            high, rest = split(value)
            middle, low = split(value - high.astype(F32))
            if side == 0:
                value = mm(picks[0], high) + mm(picks[0], middle) + mm(picks[0], low)
            else:
                value = mm(high, picks[1]) + mm(middle, picks[1]) + mm(low, picks[1])
        return value

    kernel_out[0] = reorder(wave[0])
    kernel_out[1] = reorder(wave[1])
    measured_out[...] = reorder(measured[0])


def first_kernel(place, row_off, col_off, own, halo, mine, other, prop, tables, lane, row_table,
                 moved, window, probes, mid):
    slot, core = place[0], place[2]
    cut_window(own, halo, row_off[slot], col_off[slot], window)

    def one_mode(mode, carry):
        for index, rows in enumerate(BLOCKS):
            pair = []
            for part in range(2):
                value = jnp.where(core == index, mine[mode, part], other[mode, part])
                probes[mode, part, rows, :] = value
                pair.append(value)
            real, imag = times(pair[0], pair[1], window[0, rows, :], window[1, rows, :])
            real, imag = right_forward(real, imag, tables, lane)
            mid[0, rows, :] = real
            mid[1, rows, :] = imag
        for cols in BLOCKS:
            real, imag = left_forward(mid[0, :, cols], mid[1, :, cols], tables, row_table)
            real, imag = times(prop[0, :, cols], prop[1, :, cols], real, imag)
            real, imag = left_inverse(real, imag, tables, row_table)
            moved[mode, 0, :, cols] = real
            moved[mode, 1, :, cols] = imag
        return carry

    lax.fori_loop(0, 4, one_mode, 0)


def second_kernel(place, row_off, col_off, own, halo, moved, tables, lane, row_table,
                  before, far, power, window, mid):
    slot = place[0]
    cut_window(own, halo, row_off[slot], col_off[slot], window)
    power[...] = jnp.zeros(power.shape, F32)

    def one_mode(mode, carry):
        for rows in BLOCKS:
            real, imag = right_inverse(moved[mode, 0, rows, :], moved[mode, 1, rows, :], tables, lane)
            before[mode, 0, rows, :] = real
            before[mode, 1, rows, :] = imag
            real, imag = times(real, imag, window[0, rows, :], window[1, rows, :])
            real, imag = right_forward(real, imag, tables, lane)
            mid[0, rows, :] = real
            mid[1, rows, :] = imag
        for cols in BLOCKS:
            real, imag = left_forward(mid[0, :, cols], mid[1, :, cols], tables, row_table)
            far[mode, 0, :, cols] = real
            far[mode, 1, :, cols] = imag
            power[:, cols] += real * real + imag * imag
        return carry

    lax.fori_loop(0, 4, one_mode, 0)


def third_kernel(place, row_off, col_off, counts, far, before, window0, window1, probes, prop,
                 power, power_other, measured, tables, lane, row_table,
                 pieces, keep, send, weight, mid, late, terms):
    slot, core = place[0], place[2]
    alive = jnp.where(slot < counts[0], 1.0 / MODES, 0.0).astype(F32)
    weight[...] = (power[...] + power_other[...] - measured[...]) * alive
    terms[...] = jnp.zeros(terms.shape, F32)

    def one_mode(mode, carry):
        home = lax.rem(slot - mode + 4, 4)
        for cols in BLOCKS:
            scale = weight[:, cols]
            real, imag = left_inverse(
                far[mode, 0, :, cols] * scale, far[mode, 1, :, cols] * scale, tables, row_table
            )
            mid[0, :, cols] = real
            mid[1, :, cols] = imag
        for rows in BLOCKS:
            real, imag = right_inverse(mid[0, rows, :], mid[1, rows, :], tables, lane)
            tr, ti = times_conj(before[mode, 0, rows, :], before[mode, 1, rows, :], real, imag)
            terms[1, 0, rows, :] += tr
            terms[1, 1, rows, :] += ti
            real, imag = times_conj(window1[0, rows, :], window1[1, rows, :], real, imag)
            real, imag = right_forward(real, imag, tables, lane)
            late[0, rows, :] = real
            late[1, rows, :] = imag
        for cols in BLOCKS:
            real, imag = left_forward(late[0, :, cols], late[1, :, cols], tables, row_table)
            real, imag = times_conj(prop[0, :, cols], prop[1, :, cols], real, imag)
            real, imag = left_inverse(real, imag, tables, row_table)
            mid[0, :, cols] = real
            mid[1, :, cols] = imag
        for index, rows in enumerate(BLOCKS):
            real, imag = right_inverse(mid[0, rows, :], mid[1, rows, :], tables, lane)
            tr, ti = times_conj(probes[mode, 0, rows, :], probes[mode, 1, rows, :], real, imag)
            terms[0, 0, rows, :] += tr
            terms[0, 1, rows, :] += ti
            pair = times_conj(window0[0, rows, :], window0[1, rows, :], real, imag)
            for part in range(2):
                for group in range(4):
                    upper = pair[part][group * 32 : group * 32 + 16]
                    lower = pair[part][group * 32 + 16 : group * 32 + 32]
                    keep[index * 4 + group, home, part] = jnp.where(core == 0, upper, lower)
                    send[index * 4 + group, home, part] = jnp.where(core == 0, lower, upper)
        return carry

    lax.fori_loop(0, 4, one_mode, 0)
    for layer in range(2):
        for part in range(2):
            ring = pltpu.roll(terms[layer, part], row_off[slot], 0)
            ring = pltpu.roll(ring, col_off[slot], 1)
            for shard in range(8):
                pieces[shard, layer, part] = ring[shard * 32 : shard * 32 + 32]


def gather_kernel(place, row_off, col_off, arrived, own, halo):
    shard = place[0] * 2 + place[1]
    rows = lax.broadcasted_iota(jnp.int32, (32, WIN), 0) + shard * 32
    lanes = lax.broadcasted_iota(jnp.int32, (32, HALF), 1)
    for layer in range(2):
        for part in range(2):
            mine = [jnp.zeros((32, HALF), F32) for _ in range(3)]
            next_one = [jnp.zeros((32, HALF), F32) for _ in range(3)]
            for slot in range(4):
                value = arrived[2 * slot, layer, part] + arrived[2 * slot + 1, layer, part]
                inside = rows >= row_off[slot]
                turned = lanes < col_off[slot]
                for store, kept in (
                    (mine, jnp.where(inside, value, 0.0)),
                    (next_one, jnp.where(inside, 0.0, value)),
                ):
                    first, second = kept[:, :HALF], kept[:, HALF:]
                    store[0] = store[0] + jnp.where(turned, 0.0, first)
                    store[1] = store[1] + second
                    store[2] = store[2] + jnp.where(turned, first, 0.0)
            own[layer, part] = jnp.concatenate(mine, axis=1)
            halo[layer, part] = jnp.concatenate(next_one, axis=1)


def join_kernel(place, *refs):
    out = refs[-1]
    shard = place[0] * 2 + place[1]
    for step in range(8):
        start = pl.multiple_of(lax.rem(shard - step + 8, 8) * 32, 32)
        for layer in range(2):
            for part in range(2):
                out[layer, part, pl.ds(start, 32), :] = refs[step][layer, part]


def shape(*sizes):
    return jax.ShapeDtypeStruct(sizes, F32)


def ring_route(size, step):
    return [(i, (i + step) % size) for i in range(size)]


def per_device(object_field, probe, measured, prop_phase, counts, row_offset, col_offset):
    matrices, lane_table, row_table, picks = (jnp.asarray(t) for t in make_tables())
    slot, high, core = lax.axis_index("y"), lax.axis_index("zh"), lax.axis_index("core")
    place = jnp.stack([slot, high, core]).astype(jnp.int32)
    back = [(i, i - 1) for i in range(1, 16)]
    ahead = [(i, i + 1) for i in range(15)]

    halo0 = lax.ppermute(object_field[0], TILE, back)
    half = lax.dynamic_slice_in_dim(probe[0], core * HALF, HALF, axis=1)
    gathered = [half] + [lax.ppermute(half, "y", ring_route(4, k)) for k in (1, 2, 3)]
    mine = jnp.stack(gathered)
    halo1 = lax.ppermute(object_field[1], TILE, back)
    other = lax.ppermute(mine, "core", [(0, 1), (1, 0)])

    wave = jnp.stack([jnp.cos(prop_phase), jnp.sin(prop_phase)])
    prop, target = pl.pallas_call(
        prepare_kernel,
        out_shape=(shape(2, WIN, WIN), shape(WIN, WIN)),
        grid_spec=pltpu.PrefetchScalarGridSpec(
            num_scalar_prefetch=1,
            grid=(1,),
            in_specs=[
                pl.BlockSpec((1, WIN, WIN), lambda i, p: (p[0], 0, 0)),
                pl.BlockSpec((2, WIN, WIN), lambda i, p: (0, 0, 0)),
                pl.BlockSpec((2, WIN, WIN), lambda i, p: (0, 0, 0)),
            ],
            out_specs=[
                pl.BlockSpec((2, WIN, WIN), lambda i, p: (0, 0, 0)),
                pl.BlockSpec((WIN, WIN), lambda i, p: (0, 0)),
            ],
        ),
        compiler_params=PARAMS,
        name="prepare",
    )(place, measured, wave, picks)

    moved, window0, probes = pl.pallas_call(
        first_kernel,
        out_shape=(shape(4, 2, WIN, WIN), shape(2, WIN, WIN), shape(4, 2, WIN, WIN)),
        in_specs=[SMEM] * 3 + [VMEM] * 8,
        out_specs=[VMEM] * 3,
        scratch_shapes=[pltpu.VMEM((2, WIN, WIN), F32)],
        compiler_params=PARAMS,
        name="first",
    )(place, row_offset, col_offset, object_field[0], halo0, mine, other, prop, matrices,
      lane_table, row_table)

    before, far, power, window1 = pl.pallas_call(
        second_kernel,
        out_shape=(shape(4, 2, WIN, WIN), shape(4, 2, WIN, WIN), shape(WIN, WIN),
                   shape(2, WIN, WIN)),
        in_specs=[SMEM] * 3 + [VMEM] * 6,
        out_specs=[VMEM] * 4,
        scratch_shapes=[pltpu.VMEM((2, WIN, WIN), F32)],
        compiler_params=PARAMS,
        name="second",
    )(place, row_offset, col_offset, object_field[1], halo1, moved, matrices, lane_table,
      row_table)

    power_other = lax.ppermute(power, "zh", [(0, 1), (1, 0)])

    pieces, keep, send = pl.pallas_call(
        third_kernel,
        out_shape=(shape(8, 2, 2, 32, WIN), shape(8, 4, 2, 16, WIN), shape(8, 4, 2, 16, WIN)),
        in_specs=[SMEM] * 4 + [VMEM] * 12,
        out_specs=[VMEM] * 3,
        scratch_shapes=[
            pltpu.VMEM((WIN, WIN), F32),
            pltpu.VMEM((2, WIN, WIN), F32),
            pltpu.VMEM((2, WIN, WIN), F32),
            pltpu.VMEM((2, 2, WIN, WIN), F32),
        ],
        compiler_params=PARAMS,
        name="third",
    )(place, row_offset, col_offset, counts, far, before, window0, window1, probes, prop, power,
      power_other, target, matrices, lane_table, row_table)

    swapped = lax.ppermute(send, "core", [(0, 1), (1, 0)])
    arrived = lax.all_to_all(pieces, MODE, 0, 0)
    own, over = pl.pallas_call(
        gather_kernel,
        out_shape=(shape(2, 2, 32, COLS), shape(2, 2, 32, COLS)),
        in_specs=[SMEM] * 3 + [VMEM],
        out_specs=[VMEM] * 2,
        compiler_params=PARAMS,
        name="gather",
    )(place, row_offset, col_offset, arrived)
    over_in = lax.ppermute(over, TILE, ahead)
    spread = lax.all_to_all((keep + swapped).reshape(32, 2, 16, WIN), SPREAD, 0, 0)
    probe_part = jnp.sum(spread, axis=0)

    total = own + over_in
    parts = [total] + [lax.ppermute(total, MODE, ring_route(8, k)) for k in range(1, 8)]
    probe_all = lax.all_to_all(jnp.broadcast_to(probe_part, (16, 2, 16, WIN)), TILE, 0, 0)
    object_grad = pl.pallas_call(
        join_kernel,
        out_shape=shape(2, 2, WIN, COLS),
        in_specs=[SMEM] + [VMEM] * 8,
        out_specs=VMEM,
        compiler_params=PARAMS,
        name="join",
    )(place, *parts)
    probe_grad = jnp.transpose(probe_all, (1, 0, 2, 3)).reshape(1, 2, WIN, WIN)
    return object_grad, probe_grad


def solution(mesh):
    fine = Mesh(mesh.devices.reshape(2, 4, 2, 4, 2), ("zl", "x", "core", "y", "zh"))
    placed = (
        P(None, None, TILE, None),
        P(MODE, None, None, None),
        P(TILE, None, None),
        P(),
        P(TILE),
        P(TILE),
        P(TILE),
    )
    return jax.shard_map(
        per_device,
        mesh=fine,
        in_specs=placed,
        out_specs=(P(None, None, TILE, None), P(MODE, None, None, None)),
        check_vma=False,
    )
```

```python
import functools
import math

import jax
import jax.numpy as jnp
import numpy as np
from jax import lax
from jax.experimental import pallas as pl
from jax.experimental.pallas import tpu as pltpu
from jax.sharding import Mesh, PartitionSpec as P


WIN = 256
HALF = 128
MODES = 8
COLS = 384
F32 = jnp.float32
BF16 = jnp.bfloat16
TILE = ("zl", "x", "core")
MODE = ("y", "zh")
SPREAD = ("zl", "x", "y")
VMEM = pl.BlockSpec(memory_space=pltpu.VMEM)
SMEM = pl.BlockSpec(memory_space=pltpu.SMEM)
PARAMS = pltpu.CompilerParams(vmem_limit_bytes=24 * 1024 * 1024)


def make_tables():
    index = np.arange(HALF)
    angle = (index[:, None] * index[None, :] % HALF) * (2.0 * math.pi / HALF)
    cosine, sine = np.cos(angle) / 16.0, np.sin(angle) / 16.0
    ahead = np.block([[cosine, -sine], [sine, cosine]])
    both = []
    for matrix in (ahead, ahead.T):
        high = matrix.astype(np.float32).astype(jnp.bfloat16)
        low = (matrix - high.astype(np.float64)).astype(np.float32).astype(jnp.bfloat16)
        both += [high, low]
    turn = index * (math.pi / HALF)
    lane = np.stack([np.cos(turn), np.sin(turn)])
    lane_table = np.broadcast_to(lane[:, None, :], (2, 8, HALF)).astype(np.float32)
    row_table = np.broadcast_to(lane[:, :, None], (2, HALF, HALF)).astype(np.float32)
    order = np.concatenate([np.arange(0, WIN, 2), np.arange(1, WIN, 2)])
    pick = np.zeros((WIN, WIN), np.float32)
    pick[np.arange(WIN), order] = 1.0
    picks = np.stack([pick, pick.T]).astype(jnp.bfloat16)
    return np.stack(both), lane_table, row_table, picks


def mm(left, right):
    return jnp.dot(left, right, preferred_element_type=F32)


def split(value):
    high = value.astype(BF16)
    return high, (value - high.astype(F32)).astype(BF16)


def dot_right(value, tables, which):
    high, low = split(value)
    return mm(high, tables[which]) + (mm(low, tables[which]) + mm(high, tables[which + 1]))


def dot_left(tables, which, value):
    high, low = split(value)
    return mm(tables[which], high) + (mm(tables[which], low) + mm(tables[which + 1], high))


def right_forward(real, imag, tables, lane):
    rows = real.shape[0]
    cosine, sine = lane[0, 0:1, :], lane[1, 0:1, :]
    ar, br, ai, bi = real[:, :HALF], real[:, HALF:], imag[:, :HALF], imag[:, HALF:]
    dr, di = ar - br, ai - bi
    top = jnp.concatenate([ar + br, ai + bi], axis=1)
    low = jnp.concatenate([dr * cosine + di * sine, di * cosine - dr * sine], axis=1)
    out = dot_right(jnp.concatenate([top, low], axis=0), tables, 0)
    even, odd = out[:rows], out[rows:]
    return (
        jnp.concatenate([even[:, :HALF], odd[:, :HALF]], axis=1),
        jnp.concatenate([even[:, HALF:], odd[:, HALF:]], axis=1),
    )


def right_inverse(real, imag, tables, lane):
    rows = real.shape[0]
    cosine, sine = lane[0, 0:1, :], lane[1, 0:1, :]
    even = jnp.concatenate([real[:, :HALF], imag[:, :HALF]], axis=1)
    odd = jnp.concatenate([real[:, HALF:], imag[:, HALF:]], axis=1)
    out = dot_right(jnp.concatenate([even, odd], axis=0), tables, 2)
    er, ei = out[:rows, :HALF], out[:rows, HALF:]
    pr, pi = out[rows:, :HALF], out[rows:, HALF:]
    tr, ti = pr * cosine - pi * sine, pi * cosine + pr * sine
    return (
        jnp.concatenate([er + tr, er - tr], axis=1),
        jnp.concatenate([ei + ti, ei - ti], axis=1),
    )


def left_forward(real, imag, tables, row):
    width = real.shape[1]
    cosine, sine = row[0], row[1]
    ar, br, ai, bi = real[:HALF], real[HALF:], imag[:HALF], imag[HALF:]
    dr, di = ar - br, ai - bi
    top = jnp.concatenate([ar + br, ai + bi], axis=0)
    low = jnp.concatenate([dr * cosine + di * sine, di * cosine - dr * sine], axis=0)
    out = dot_left(tables, 2, jnp.concatenate([top, low], axis=1))
    even, odd = out[:, :width], out[:, width:]
    return (
        jnp.concatenate([even[:HALF], odd[:HALF]], axis=0),
        jnp.concatenate([even[HALF:], odd[HALF:]], axis=0),
    )


def left_inverse(real, imag, tables, row):
    width = real.shape[1]
    cosine, sine = row[0], row[1]
    even = jnp.concatenate([real[:HALF], imag[:HALF]], axis=0)
    odd = jnp.concatenate([real[HALF:], imag[HALF:]], axis=0)
    out = dot_left(tables, 0, jnp.concatenate([even, odd], axis=1))
    er, ei = out[:HALF, :width], out[HALF:, :width]
    pr, pi = out[:HALF, width:], out[HALF:, width:]
    tr, ti = pr * cosine - pi * sine, pi * cosine + pr * sine
    return (
        jnp.concatenate([er + tr, er - tr], axis=0),
        jnp.concatenate([ei + ti, ei - ti], axis=0),
    )


def times(ar, ai, br, bi):
    return ar * br - ai * bi, ar * bi + ai * br


def times_conj(ar, ai, br, bi):
    return ar * br + ai * bi, ar * bi - ai * br


BLOCKS = (slice(0, HALF), slice(HALF, WIN))


def cut_window(own, halo, row, col, out):
    rows = lax.broadcasted_iota(jnp.int32, (WIN, COLS), 0)
    lanes = lax.broadcasted_iota(jnp.int32, (WIN, HALF), 1)
    for part in range(2):
        chosen = jnp.where(rows < row, halo[part], own[part])
        first = jnp.where(lanes < col, chosen[:, 2 * HALF :], chosen[:, :HALF])
        ring = jnp.concatenate([first, chosen[:, HALF : 2 * HALF]], axis=1)
        ring = pltpu.roll(ring, lax.rem(WIN - row, WIN), 0)
        out[part] = pltpu.roll(ring, lax.rem(WIN - col, WIN), 1)


def prepare_kernel(place, measured, wave, picks, kernel_out, measured_out):
    def reorder(value):
        for side in range(2):
            high, _ = split(value)
            middle, low = split(value - high.astype(F32))
            if side == 0:
                value = mm(picks[0], high) + mm(picks[0], middle) + mm(picks[0], low)
            else:
                value = mm(high, picks[1]) + mm(middle, picks[1]) + mm(low, picks[1])
        return value

    kernel_out[0] = reorder(wave[0])
    kernel_out[1] = reorder(wave[1])
    measured_out[...] = reorder(measured[0])


def spread_mode(pair, window, prop, tables, lane, row_table, mid, out):
    for rows in BLOCKS:
        real, imag = pair(rows)
        real, imag = times(real, imag, window[0, rows, :], window[1, rows, :])
        real, imag = right_forward(real, imag, tables, lane)
        mid[0, rows, :] = real
        mid[1, rows, :] = imag
    for cols in BLOCKS:
        real, imag = left_forward(mid[0, :, cols], mid[1, :, cols], tables, row_table)
        real, imag = times(prop[0, :, cols], prop[1, :, cols], real, imag)
        real, imag = left_inverse(real, imag, tables, row_table)
        out[0, :, cols] = real
        out[1, :, cols] = imag


def start_kernel(place, row_off, col_off, own, halo, probe, prop, tables, lane, row_table,
                 moved, probes, window, mid):
    slot = place[0]
    cut_window(own.at[0], halo, row_off[slot], col_off[slot], window)
    probes[0] = probe[0]
    spread_mode(lambda rows: (probe[0, 0, rows, :], probe[0, 1, rows, :]), window, prop, tables,
                lane, row_table, mid, moved.at[0])


def first_kernel(place, window, mine, other, prop, tables, lane, row_table, moved_in, probes_in,
                 moved, probes, mid):
    core = place[2]

    def pair(rows):
        index = BLOCKS.index(rows)
        values = []
        for part in range(2):
            value = jnp.where(core == index, mine[0, part], other[0, part])
            probes[0, part, rows, :] = value
            values.append(value)
        return values

    spread_mode(pair, window, prop, tables, lane, row_table, mid, moved.at[0])


def second_kernel(place, row_off, col_off, own, halo, moved, tables, lane, row_table,
                  before, far, power, window, mid):
    slot = place[0]

    @pl.when(pl.program_id(0) == 0)
    def _():
        cut_window(own.at[0], halo, row_off[slot], col_off[slot], window)
        power[...] = jnp.zeros(power.shape, F32)

    for rows in BLOCKS:
        real, imag = right_inverse(moved[0, 0, rows, :], moved[0, 1, rows, :], tables, lane)
        before[0, 0, rows, :] = real
        before[0, 1, rows, :] = imag
        real, imag = times(real, imag, window[0, rows, :], window[1, rows, :])
        real, imag = right_forward(real, imag, tables, lane)
        mid[0, rows, :] = real
        mid[1, rows, :] = imag
    for cols in BLOCKS:
        real, imag = left_forward(mid[0, :, cols], mid[1, :, cols], tables, row_table)
        far[0, 0, :, cols] = real
        far[0, 1, :, cols] = imag
        power[:, cols] += real * real + imag * imag


def third_kernel(place, row_off, col_off, counts, far, before, window0, window1, probes, prop,
                 power, power_other, measured, tables, lane, row_table,
                 pieces, keep, send, weight, mid, late, terms):
    slot, core = place[0], place[2]

    @pl.when(pl.program_id(0) == 0)
    def _():
        alive = jnp.where(slot < counts[0], 1.0 / MODES, 0.0).astype(F32)
        weight[...] = (power[...] + power_other[...] - measured[...]) * alive
        terms[...] = jnp.zeros(terms.shape, F32)

    for cols in BLOCKS:
        scale = weight[:, cols]
        real, imag = left_inverse(
            far[0, 0, :, cols] * scale, far[0, 1, :, cols] * scale, tables, row_table
        )
        mid[0, :, cols] = real
        mid[1, :, cols] = imag
    for rows in BLOCKS:
        real, imag = right_inverse(mid[0, rows, :], mid[1, rows, :], tables, lane)
        tr, ti = times_conj(before[0, 0, rows, :], before[0, 1, rows, :], real, imag)
        terms[1, 0, rows, :] += tr
        terms[1, 1, rows, :] += ti
        real, imag = times_conj(window1[0, rows, :], window1[1, rows, :], real, imag)
        real, imag = right_forward(real, imag, tables, lane)
        late[0, rows, :] = real
        late[1, rows, :] = imag
    for cols in BLOCKS:
        real, imag = left_forward(late[0, :, cols], late[1, :, cols], tables, row_table)
        real, imag = times_conj(prop[0, :, cols], prop[1, :, cols], real, imag)
        real, imag = left_inverse(real, imag, tables, row_table)
        mid[0, :, cols] = real
        mid[1, :, cols] = imag
    for index, rows in enumerate(BLOCKS):
        real, imag = right_inverse(mid[0, rows, :], mid[1, rows, :], tables, lane)
        tr, ti = times_conj(probes[0, 0, rows, :], probes[0, 1, rows, :], real, imag)
        terms[0, 0, rows, :] += tr
        terms[0, 1, rows, :] += ti
        pair = times_conj(window0[0, rows, :], window0[1, rows, :], real, imag)
        for part in range(2):
            for group in range(4):
                upper = pair[part][group * 32 : group * 32 + 16]
                lower = pair[part][group * 32 + 16 : group * 32 + 32]
                keep[index * 4 + group, 0, part] = jnp.where(core == 0, upper, lower)
                send[index * 4 + group, 0, part] = jnp.where(core == 0, lower, upper)

    @pl.when(pl.program_id(0) == 3)
    def _():
        for layer in range(2):
            for part in range(2):
                ring = pltpu.roll(terms[layer, part], row_off[slot], 0)
                ring = pltpu.roll(ring, col_off[slot], 1)
                for shard in range(8):
                    pieces[shard, layer, part] = ring[shard * 32 : shard * 32 + 32]


def gather_kernel(place, row_off, col_off, arrived, own, halo):
    shard = place[0] * 2 + place[1]
    rows = lax.broadcasted_iota(jnp.int32, (32, WIN), 0) + shard * 32
    lanes = lax.broadcasted_iota(jnp.int32, (32, HALF), 1)
    for layer in range(2):
        for part in range(2):
            mine = [jnp.zeros((32, HALF), F32) for _ in range(3)]
            next_one = [jnp.zeros((32, HALF), F32) for _ in range(3)]
            for slot in range(4):
                value = arrived[2 * slot, layer, part] + arrived[2 * slot + 1, layer, part]
                inside = rows >= row_off[slot]
                turned = lanes < col_off[slot]
                for store, kept in (
                    (mine, jnp.where(inside, value, 0.0)),
                    (next_one, jnp.where(inside, 0.0, value)),
                ):
                    first, second = kept[:, :HALF], kept[:, HALF:]
                    store[0] = store[0] + jnp.where(turned, 0.0, first)
                    store[1] = store[1] + second
                    store[2] = store[2] + jnp.where(turned, first, 0.0)
            own[layer, part] = jnp.concatenate(mine, axis=1)
            halo[layer, part] = jnp.concatenate(next_one, axis=1)


def join_kernel(first, last, place, *refs):
    out, sem = refs[-2], refs[-1]
    shard = place[0] * 2 + place[1]
    copies = []
    for step in range(first, last):
        start = pl.multiple_of(lax.rem(shard - step + 8, 8) * 32, 32)
        copies.append(
            pltpu.make_async_copy(
                refs[step - first], out.at[:, :, pl.ds(start, 32), :], sem.at[step]
            )
        )
    for copy in copies:
        copy.start()
    for copy in copies:
        copy.wait()


def whole(*sizes):
    return pl.BlockSpec(sizes, lambda *_: (0,) * len(sizes))


def by_mode(*sizes):
    return pl.BlockSpec((1,) + sizes, lambda i, *_: (i,) + (0,) * len(sizes))


def by_home():
    return pl.BlockSpec(
        (8, 1, 2, 16, WIN), lambda i, place, *_: (0, lax.rem(place[0] - i + 4, 4), 0, 0, 0)
    )


TABLES = [whole(4, WIN, WIN), whole(2, 8, HALF), whole(2, HALF, HALF)]
PLANE = whole(WIN, WIN)
FIELD = whole(2, WIN, WIN)
MODAL = by_mode(2, WIN, WIN)
STRIP = whole(2, WIN, COLS)


def layer_of(layer):
    return pl.BlockSpec((1, 2, WIN, COLS), lambda *_: (layer, 0, 0, 0))


ANY = pl.BlockSpec(memory_space=pl.ANY)


def modal_call(body, scalars, steps, ins, outs, out_shape, scratch, aliases=None):
    return pl.pallas_call(
        body,
        out_shape=out_shape,
        grid_spec=pltpu.PrefetchScalarGridSpec(
            num_scalar_prefetch=scalars,
            grid=(steps,),
            in_specs=ins,
            out_specs=outs,
            scratch_shapes=scratch,
        ),
        input_output_aliases=aliases or {},
        compiler_params=PARAMS,
    )


def shape(*sizes):
    return jax.ShapeDtypeStruct(sizes, F32)


def ring_route(size, step):
    return [(i, (i + step) % size) for i in range(size)]


def per_device(object_field, probe, measured, prop_phase, counts, row_offset, col_offset):
    matrices, lane_table, row_table, picks = (jnp.asarray(t) for t in make_tables())
    slot, high, core = lax.axis_index("y"), lax.axis_index("zh"), lax.axis_index("core")
    place = jnp.stack([slot, high, core]).astype(jnp.int32)
    back = [(i, i - 1) for i in range(1, 16)]
    ahead = [(i, i + 1) for i in range(15)]

    halo0 = lax.ppermute(object_field[0], TILE, back)
    half = lax.dynamic_slice_in_dim(probe[0], core * HALF, HALF, axis=1)
    gathered = []
    for k in (1, 2, 3):
        gathered.append(lax.ppermute(half, "y", ring_route(4, k)))
    later, half = lax.optimization_barrier((object_field, half))
    halo1 = lax.ppermute(later[1], TILE, back)
    swap = [(0, 1), (1, 0)]
    mine13 = jnp.stack([gathered[0], gathered[2]])
    mine2 = gathered[1][None]
    other13 = lax.ppermute(mine13, "core", swap)
    other2 = lax.ppermute(mine2, "core", swap)

    wave = jnp.stack([jnp.cos(prop_phase), jnp.sin(prop_phase)])
    prop, target = pl.pallas_call(
        prepare_kernel,
        out_shape=(shape(2, WIN, WIN), shape(WIN, WIN)),
        grid_spec=pltpu.PrefetchScalarGridSpec(
            num_scalar_prefetch=1,
            grid=(1,),
            in_specs=[
                pl.BlockSpec((1, WIN, WIN), lambda i, p: (p[0], 0, 0)), FIELD, FIELD
            ],
            out_specs=[FIELD, PLANE],
        ),
        compiler_params=PARAMS,
        name="prepare",
    )(place, measured, wave, picks)

    modes = shape(4, 2, WIN, WIN)
    tables = (matrices, lane_table, row_table)
    work = [pltpu.VMEM((2, WIN, WIN), F32)]
    moved, probes, window0 = modal_call(
        start_kernel, 3, 1,
        [layer_of(0), STRIP, MODAL, FIELD] + TABLES,
        [MODAL, MODAL, FIELD], (modes, modes, shape(2, WIN, WIN)), work,
    )(place, row_offset, col_offset, object_field, halo0, probe, prop, *tables)
    for base, mine, other in ((1, mine13, other13), (2, mine2, other2)):
        target_block = pl.BlockSpec(
            (1, 2, WIN, WIN), lambda i, *_, base=base: (base + 2 * i, 0, 0, 0)
        )
        moved, probes = modal_call(
            first_kernel, 1, mine.shape[0],
            [FIELD, by_mode(2, HALF, WIN), by_mode(2, HALF, WIN), FIELD] + TABLES + [ANY, ANY],
            [target_block, target_block], (modes, modes), work, {8: 0, 9: 1},
        )(place, window0, mine, other, prop, *tables, moved, probes)

    before, far, power, window1 = modal_call(
        second_kernel, 3, 4,
        [layer_of(1), STRIP, MODAL] + TABLES,
        [MODAL, MODAL, PLANE, FIELD],
        (modes, modes, shape(WIN, WIN), shape(2, WIN, WIN)),
        work,
    )(place, row_offset, col_offset, object_field, halo1, moved, *tables)

    power_other = lax.ppermute(power, "zh", [(0, 1), (1, 0)])

    parts_shape = shape(8, 4, 2, 16, WIN)
    pieces, keep, send = modal_call(
        third_kernel, 4, 4,
        [MODAL, MODAL, FIELD, FIELD, MODAL, FIELD, PLANE, PLANE, PLANE] + TABLES,
        [whole(8, 2, 2, 32, WIN), by_home(), by_home()],
        (shape(8, 2, 2, 32, WIN), parts_shape, parts_shape),
        [
            pltpu.VMEM((WIN, WIN), F32),
            pltpu.VMEM((2, WIN, WIN), F32),
            pltpu.VMEM((2, WIN, WIN), F32),
            pltpu.VMEM((2, 2, WIN, WIN), F32),
        ],
    )(place, row_offset, col_offset, counts, far, before, window0, window1, probes, prop, power,
      power_other, target, *tables)

    swapped = lax.ppermute(send, "core", [(0, 1), (1, 0)])
    arrived = lax.all_to_all(pieces, MODE, 0, 0)
    own, over = pl.pallas_call(
        gather_kernel,
        out_shape=(shape(2, 2, 32, COLS), shape(2, 2, 32, COLS)),
        in_specs=[SMEM] * 3 + [VMEM],
        out_specs=[VMEM] * 2,
        compiler_params=PARAMS,
        name="gather",
    )(place, row_offset, col_offset, arrived)
    over_in = lax.ppermute(over, TILE, ahead)
    spread = lax.all_to_all((keep + swapped).reshape(32, 2, 16, WIN), SPREAD, 0, 0)
    probe_part = jnp.sum(spread, axis=0)

    total = own + over_in
    parts = []
    for k in range(1, 8):
        parts.append(lax.ppermute(total, MODE, ring_route(8, k)))
    probe_all = lax.all_to_all(jnp.broadcast_to(probe_part, (16, 2, 16, WIN)), TILE, 0, 0)
    object_grad = pl.pallas_call(
        functools.partial(join_kernel, 0, 1),
        out_shape=shape(2, 2, WIN, COLS),
        in_specs=[SMEM, VMEM],
        out_specs=ANY,
        scratch_shapes=[pltpu.SemaphoreType.DMA((8,))],
        compiler_params=PARAMS,
        name="joina",
    )(place, total)
    object_grad = pl.pallas_call(
        functools.partial(join_kernel, 1, 8),
        out_shape=shape(2, 2, WIN, COLS),
        in_specs=[SMEM] + [VMEM] * 7 + [ANY],
        out_specs=ANY,
        scratch_shapes=[pltpu.SemaphoreType.DMA((8,))],
        input_output_aliases={8: 0},
        compiler_params=PARAMS,
        name="joinb",
    )(place, *parts, object_grad)
    probe_grad = jnp.transpose(probe_all, (1, 0, 2, 3)).reshape(1, 2, WIN, WIN)
    return object_grad, probe_grad


def solution(mesh):
    fine = Mesh(mesh.devices.reshape(2, 4, 2, 4, 2), ("zl", "x", "core", "y", "zh"))
    placed = (
        P(None, None, TILE, None),
        P(MODE, None, None, None),
        P(TILE, None, None),
        P(),
        P(TILE),
        P(TILE),
        P(TILE),
    )

    return jax.shard_map(
        per_device,
        mesh=fine,
        in_specs=placed,
        out_specs=(P(None, None, TILE, None), P(MODE, None, None, None)),
        check_vma=False,
    )
```

```python
import functools
import math

import jax
import jax.numpy as jnp
import numpy as np
from jax import lax
from jax.experimental import pallas as pl
from jax.experimental.pallas import tpu as pltpu
from jax.sharding import Mesh, PartitionSpec as P


WIN = 256
HALF = 128
MODES = 8
COLS = 384
F32 = jnp.float32
BF16 = jnp.bfloat16
TILE = ("zl", "x", "core")
MODE = ("y", "zh")
SPREAD = ("zl", "x", "y")
VMEM = pl.BlockSpec(memory_space=pltpu.VMEM)
HBM = pl.BlockSpec(memory_space=pltpu.HBM)
SMEM = pl.BlockSpec(memory_space=pltpu.SMEM)
PARAMS = pltpu.CompilerParams(vmem_limit_bytes=24 * 1024 * 1024)


def make_tables():
    index = np.arange(HALF)
    angle = (index[:, None] * index[None, :] % HALF) * (2.0 * math.pi / HALF)
    cosine, sine = np.cos(angle) / 16.0, np.sin(angle) / 16.0
    ahead = np.block([[cosine, -sine], [sine, cosine]])
    both = []
    for matrix in (ahead, ahead.T):
        high = matrix.astype(np.float32).astype(jnp.bfloat16)
        low = (matrix - high.astype(np.float64)).astype(np.float32).astype(jnp.bfloat16)
        both += [high, low]
    turn = index * (math.pi / HALF)
    lane = np.stack([np.cos(turn), np.sin(turn)])
    lane_table = np.broadcast_to(lane[:, None, :], (2, 8, HALF)).astype(np.float32)
    row_table = np.broadcast_to(lane[:, :, None], (2, HALF, HALF)).astype(np.float32)
    order = np.concatenate([np.arange(0, WIN, 2), np.arange(1, WIN, 2)])
    pick = np.zeros((WIN, WIN), np.float32)
    pick[np.arange(WIN), order] = 1.0
    picks = np.stack([pick, pick.T]).astype(jnp.bfloat16)
    return np.stack(both), lane_table, row_table, picks


def mm(left, right):
    return jnp.dot(left, right, preferred_element_type=F32)


def split(value):
    high = value.astype(BF16)
    return high, (value - high.astype(F32)).astype(BF16)


def dot_right(value, tables, which):
    high, low = split(value)
    return mm(high, tables[which]) + (mm(low, tables[which]) + mm(high, tables[which + 1]))


def dot_left(tables, which, value):
    high, low = split(value)
    return mm(tables[which], high) + (mm(tables[which], low) + mm(tables[which + 1], high))


def right_forward(real, imag, tables, lane):
    rows = real.shape[0]
    cosine, sine = lane[0, 0:1, :], lane[1, 0:1, :]
    ar, br, ai, bi = real[:, :HALF], real[:, HALF:], imag[:, :HALF], imag[:, HALF:]
    dr, di = ar - br, ai - bi
    top = jnp.concatenate([ar + br, ai + bi], axis=1)
    low = jnp.concatenate([dr * cosine + di * sine, di * cosine - dr * sine], axis=1)
    out = dot_right(jnp.concatenate([top, low], axis=0), tables, 0)
    even, odd = out[:rows], out[rows:]
    return (
        jnp.concatenate([even[:, :HALF], odd[:, :HALF]], axis=1),
        jnp.concatenate([even[:, HALF:], odd[:, HALF:]], axis=1),
    )


def right_inverse(real, imag, tables, lane):
    rows = real.shape[0]
    cosine, sine = lane[0, 0:1, :], lane[1, 0:1, :]
    even = jnp.concatenate([real[:, :HALF], imag[:, :HALF]], axis=1)
    odd = jnp.concatenate([real[:, HALF:], imag[:, HALF:]], axis=1)
    out = dot_right(jnp.concatenate([even, odd], axis=0), tables, 2)
    er, ei = out[:rows, :HALF], out[:rows, HALF:]
    pr, pi = out[rows:, :HALF], out[rows:, HALF:]
    tr, ti = pr * cosine - pi * sine, pi * cosine + pr * sine
    return (
        jnp.concatenate([er + tr, er - tr], axis=1),
        jnp.concatenate([ei + ti, ei - ti], axis=1),
    )


def left_forward(real, imag, tables, row):
    width = real.shape[1]
    cosine, sine = row[0], row[1]
    ar, br, ai, bi = real[:HALF], real[HALF:], imag[:HALF], imag[HALF:]
    dr, di = ar - br, ai - bi
    top = jnp.concatenate([ar + br, ai + bi], axis=0)
    low = jnp.concatenate([dr * cosine + di * sine, di * cosine - dr * sine], axis=0)
    out = dot_left(tables, 2, jnp.concatenate([top, low], axis=1))
    even, odd = out[:, :width], out[:, width:]
    return (
        jnp.concatenate([even[:HALF], odd[:HALF]], axis=0),
        jnp.concatenate([even[HALF:], odd[HALF:]], axis=0),
    )


def left_inverse(real, imag, tables, row):
    width = real.shape[1]
    cosine, sine = row[0], row[1]
    even = jnp.concatenate([real[:HALF], imag[:HALF]], axis=0)
    odd = jnp.concatenate([real[HALF:], imag[HALF:]], axis=0)
    out = dot_left(tables, 0, jnp.concatenate([even, odd], axis=1))
    er, ei = out[:HALF, :width], out[HALF:, :width]
    pr, pi = out[:HALF, width:], out[HALF:, width:]
    tr, ti = pr * cosine - pi * sine, pi * cosine + pr * sine
    return (
        jnp.concatenate([er + tr, er - tr], axis=0),
        jnp.concatenate([ei + ti, ei - ti], axis=0),
    )


def times(ar, ai, br, bi):
    return ar * br - ai * bi, ar * bi + ai * br


def times_conj(ar, ai, br, bi):
    return ar * br + ai * bi, ar * bi - ai * br


BLOCKS = (slice(0, HALF), slice(HALF, WIN))


def cut_window(own, halo, row, col, out):
    rows = lax.broadcasted_iota(jnp.int32, (WIN, COLS), 0)
    lanes = lax.broadcasted_iota(jnp.int32, (WIN, HALF), 1)
    for part in range(2):
        chosen = jnp.where(rows < row, halo[part], own[part])
        first = jnp.where(lanes < col, chosen[:, 2 * HALF :], chosen[:, :HALF])
        ring = jnp.concatenate([first, chosen[:, HALF : 2 * HALF]], axis=1)
        ring = pltpu.roll(ring, lax.rem(WIN - row, WIN), 0)
        out[part] = pltpu.roll(ring, lax.rem(WIN - col, WIN), 1)


def reorder(value, picks):
    for side in range(2):
        high, _ = split(value)
        middle, low = split(value - high.astype(F32))
        if side == 0:
            value = mm(picks[0], high) + mm(picks[0], middle) + mm(picks[0], low)
        else:
            value = mm(high, picks[1]) + mm(middle, picks[1]) + mm(low, picks[1])
    return value


def prepare_kernel(phase, picks, out):
    angle = reorder(phase[...], picks)
    out[0] = jnp.cos(angle)
    out[1] = jnp.sin(angle)


def target_kernel(place, measured, picks, out):
    out[...] = reorder(measured[0], picks)


def cut_kernel(place, field, probe, layer0, layer1, half, sem):
    start = pl.multiple_of(place[2] * HALF, HALF)
    copies = (
        pltpu.make_async_copy(field.at[0], layer0, sem.at[0]),
        pltpu.make_async_copy(probe.at[0, :, pl.ds(start, HALF), :], half, sem.at[1]),
        pltpu.make_async_copy(field.at[1], layer1, sem.at[2]),
    )
    for copy in copies:
        copy.start()
    for copy in copies:
        copy.wait()


def spread_mode(pair, window, prop, tables, lane, row_table, mid, out):
    for rows in BLOCKS:
        real, imag = pair(rows)
        real, imag = times(real, imag, window[0, rows, :], window[1, rows, :])
        real, imag = right_forward(real, imag, tables, lane)
        mid[0, rows, :] = real
        mid[1, rows, :] = imag
    for cols in BLOCKS:
        real, imag = left_forward(mid[0, :, cols], mid[1, :, cols], tables, row_table)
        real, imag = times(prop[0, :, cols], prop[1, :, cols], real, imag)
        real, imag = left_inverse(real, imag, tables, row_table)
        out[0, :, cols] = real
        out[1, :, cols] = imag


def start_kernel(place, row_off, col_off, own, halo, probe, prop, tables, lane, row_table,
                 moved, probes, window, mid):
    slot = place[0]
    cut_window(own, halo, row_off[slot], col_off[slot], window)
    probes[0] = probe[0]
    spread_mode(lambda rows: (probe[0, 0, rows, :], probe[0, 1, rows, :]), window, prop, tables,
                lane, row_table, mid, moved.at[0])


def first_kernel(count, place, window, *refs):
    mine, other = refs[:count], refs[count : 2 * count]
    prop, tables, lane, row_table, _, _, moved, probes, mid = refs[2 * count :]
    core, step = place[2], pl.program_id(0)

    def pair(rows):
        index = BLOCKS.index(rows)
        values = []
        for part in range(2):
            value = jnp.where(core == index, mine[0][part], other[0][part])
            if count == 2:
                later = jnp.where(core == index, mine[1][part], other[1][part])
                value = jnp.where(step == 0, value, later)
            probes[0, part, rows, :] = value
            values.append(value)
        return values

    spread_mode(pair, window, prop, tables, lane, row_table, mid, moved.at[0])


def second_kernel(place, row_off, col_off, own, halo, moved, tables, lane, row_table,
                  before, far, power, window, mid):
    slot = place[0]

    @pl.when(pl.program_id(0) == 0)
    def _():
        cut_window(own, halo, row_off[slot], col_off[slot], window)
        power[...] = jnp.zeros(power.shape, F32)

    for rows in BLOCKS:
        real, imag = right_inverse(moved[0, 0, rows, :], moved[0, 1, rows, :], tables, lane)
        before[0, 0, rows, :] = real
        before[0, 1, rows, :] = imag
        real, imag = times(real, imag, window[0, rows, :], window[1, rows, :])
        real, imag = right_forward(real, imag, tables, lane)
        mid[0, rows, :] = real
        mid[1, rows, :] = imag
    for cols in BLOCKS:
        real, imag = left_forward(mid[0, :, cols], mid[1, :, cols], tables, row_table)
        far[0, 0, :, cols] = real
        far[0, 1, :, cols] = imag
        power[:, cols] += real * real + imag * imag


def third_kernel(place, row_off, col_off, counts, far, before, window0, window1, probes, prop,
                 power, power_other, measured, tables, lane, row_table,
                 *rest):
    pieces, (keep, send, weight, mid, late, terms) = rest[:8], rest[8:]
    slot, core = place[0], place[2]

    @pl.when(pl.program_id(0) == 0)
    def _():
        alive = jnp.where(slot < counts[0], 1.0 / MODES, 0.0).astype(F32)
        weight[...] = (power[...] + power_other[...] - measured[...]) * alive
        terms[...] = jnp.zeros(terms.shape, F32)

    for cols in BLOCKS:
        scale = weight[:, cols]
        real, imag = left_inverse(
            far[0, 0, :, cols] * scale, far[0, 1, :, cols] * scale, tables, row_table
        )
        mid[0, :, cols] = real
        mid[1, :, cols] = imag
    for rows in BLOCKS:
        real, imag = right_inverse(mid[0, rows, :], mid[1, rows, :], tables, lane)
        tr, ti = times_conj(before[0, 0, rows, :], before[0, 1, rows, :], real, imag)
        terms[1, 0, rows, :] += tr
        terms[1, 1, rows, :] += ti
        real, imag = times_conj(window1[0, rows, :], window1[1, rows, :], real, imag)
        real, imag = right_forward(real, imag, tables, lane)
        late[0, rows, :] = real
        late[1, rows, :] = imag
    for cols in BLOCKS:
        real, imag = left_forward(late[0, :, cols], late[1, :, cols], tables, row_table)
        real, imag = times_conj(prop[0, :, cols], prop[1, :, cols], real, imag)
        real, imag = left_inverse(real, imag, tables, row_table)
        mid[0, :, cols] = real
        mid[1, :, cols] = imag
    for index, rows in enumerate(BLOCKS):
        real, imag = right_inverse(mid[0, rows, :], mid[1, rows, :], tables, lane)
        tr, ti = times_conj(probes[0, 0, rows, :], probes[0, 1, rows, :], real, imag)
        terms[0, 0, rows, :] += tr
        terms[0, 1, rows, :] += ti
        pair = times_conj(window0[0, rows, :], window0[1, rows, :], real, imag)
        for part in range(2):
            for group in range(4):
                upper = pair[part][group * 32 : group * 32 + 16]
                lower = pair[part][group * 32 + 16 : group * 32 + 32]
                keep[index * 4 + group, 0, part] = jnp.where(core == 0, upper, lower)
                send[index * 4 + group, 0, part] = jnp.where(core == 0, lower, upper)

    @pl.when(pl.program_id(0) == 3)
    def _():
        for layer in range(2):
            for part in range(2):
                ring = pltpu.roll(terms[layer, part], row_off[slot], 0)
                terms[layer, part] = pltpu.roll(ring, col_off[slot], 1)
        shard = place[0] * 2 + place[1]
        for step in range(8):
            start = pl.multiple_of(lax.rem(shard + step, 8) * 32, 32)
            for layer in range(2):
                for part in range(2):
                    pieces[step][layer, part] = terms[layer, part, pl.ds(start, 32), :]


def gather_kernel(place, row_off, col_off, *refs):
    arrived, (own, halo) = refs[:8], refs[8:]
    shard = place[0] * 2 + place[1]
    rows = lax.broadcasted_iota(jnp.int32, (32, HALF), 0) + shard * 32
    lanes = lax.broadcasted_iota(jnp.int32, (32, HALF), 1)
    for layer in range(2):
        for part in range(2):
            mine = [jnp.zeros((32, HALF), F32) for _ in range(3)]
            next_one = [jnp.zeros((32, HALF), F32) for _ in range(3)]
            for step in range(8):
                slot = lax.div(lax.rem(shard - step + 8, 8), 2)
                value = arrived[step][layer, part]
                first, second = value[:, :HALF], value[:, HALF:]
                inside = rows >= row_off[slot]
                turned = lanes < col_off[slot]
                moves = (jnp.where(turned, 0.0, first), second, jnp.where(turned, first, 0.0))
                for place_in, move in enumerate(moves):
                    mine[place_in] = mine[place_in] + jnp.where(inside, move, 0.0)
                    next_one[place_in] = next_one[place_in] + jnp.where(inside, 0.0, move)
            own[layer, part] = jnp.concatenate(mine, axis=1)
            halo[layer, part] = jnp.concatenate(next_one, axis=1)


def join_kernel(first, last, place, *refs):
    out, sem = refs[-2], refs[-1]
    shard = place[0] * 2 + place[1]
    copies = []
    for step in range(first, last):
        start = pl.multiple_of(lax.rem(shard - step + 8, 8) * 32, 32)
        copies.append(
            pltpu.make_async_copy(
                refs[step - first], out.at[:, :, pl.ds(start, 32), :], sem.at[step]
            )
        )
    for copy in copies:
        copy.start()
    for copy in copies:
        copy.wait()


def whole(*sizes):
    return pl.BlockSpec(sizes, lambda *_: (0,) * len(sizes))


def by_mode(*sizes):
    return pl.BlockSpec((1,) + sizes, lambda i, *_: (i,) + (0,) * len(sizes))


def by_home():
    return pl.BlockSpec(
        (8, 1, 2, 16, WIN), lambda i, place, *_: (0, lax.rem(place[0] - i + 4, 4), 0, 0, 0)
    )


TABLES = [VMEM, VMEM, VMEM]
PLANE = whole(WIN, WIN)
FIELD = whole(2, WIN, WIN)
MODAL = by_mode(2, WIN, WIN)
STRIP = whole(2, WIN, COLS)


ANY = pl.BlockSpec(memory_space=pl.ANY)


def modal_call(body, scalars, steps, ins, outs, out_shape, scratch, aliases=None):
    return pl.pallas_call(
        body,
        out_shape=out_shape,
        grid_spec=pltpu.PrefetchScalarGridSpec(
            num_scalar_prefetch=scalars,
            grid=(steps,),
            in_specs=ins,
            out_specs=outs,
            scratch_shapes=scratch,
        ),
        input_output_aliases=aliases or {},
        compiler_params=PARAMS,
    )


def shape(*sizes):
    return jax.ShapeDtypeStruct(sizes, F32)


def ring_route(size, step):
    return [(i, (i + step) % size) for i in range(size)]


def per_device(object_field, probe, measured, prop_phase, counts, row_offset, col_offset):
    matrices, lane_table, row_table, picks = (jnp.asarray(t) for t in make_tables())
    slot, high, core = lax.axis_index("y"), lax.axis_index("zh"), lax.axis_index("core")
    place = jnp.stack([slot, high, core]).astype(jnp.int32)
    back = [(i, i - 1) for i in range(1, 16)]
    ahead = [(i, i + 1) for i in range(15)]

    layer0, layer1, half = pl.pallas_call(
        cut_kernel,
        out_shape=(shape(2, WIN, COLS), shape(2, WIN, COLS), shape(2, HALF, WIN)),
        in_specs=[SMEM, HBM, HBM],
        out_specs=[VMEM] * 3,
        scratch_shapes=[pltpu.SemaphoreType.DMA((3,))],
        compiler_params=PARAMS,
        name="cut",
    )(place, *(pltpu.with_memory_space_constraint(v, pltpu.HBM) for v in (object_field, probe)))
    halo0 = lax.ppermute(layer0, TILE, back)
    halo1 = lax.ppermute(layer1, TILE, back)
    swap = [(0, 1), (1, 0)]
    mine, other = {}, {}
    for k in (1, 3, 2):
        mine[k] = lax.ppermute(half, "y", ring_route(4, k))
        other[k] = lax.ppermute(mine[k], "core", swap)

    prop = pl.pallas_call(
        prepare_kernel,
        out_shape=shape(2, WIN, WIN),
        in_specs=[VMEM, VMEM],
        out_specs=VMEM,
        compiler_params=PARAMS,
        name="prepare",
    )(prop_phase, picks)
    target = pl.pallas_call(
        target_kernel,
        out_shape=shape(WIN, WIN),
        grid_spec=pltpu.PrefetchScalarGridSpec(
            num_scalar_prefetch=1,
            grid=(1,),
            in_specs=[pl.BlockSpec((1, WIN, WIN), lambda i, p: (p[0], 0, 0)), VMEM],
            out_specs=PLANE,
        ),
        compiler_params=PARAMS,
        name="target",
    )(place, measured, picks)

    modes = shape(4, 2, WIN, WIN)
    tables = (matrices, lane_table, row_table)
    work = [pltpu.VMEM((2, WIN, WIN), F32)]
    moved, probes, window0 = modal_call(
        start_kernel, 3, 1,
        [STRIP, STRIP, MODAL, FIELD] + TABLES,
        [MODAL, MODAL, FIELD], (modes, modes, shape(2, WIN, WIN)), work,
    )(place, row_offset, col_offset, layer0, halo0, probe, prop, *tables)
    for steps in ((1, 3), (2,)):
        count = len(steps)
        target_block = pl.BlockSpec(
            (1, 2, WIN, WIN), lambda i, *_, base=steps[0]: (base + 2 * i, 0, 0, 0)
        )
        moved, probes = modal_call(
            functools.partial(first_kernel, count), 1, count,
            [VMEM] * (2 * count + 2) + TABLES + [ANY, ANY],
            [target_block, target_block], (modes, modes), work,
            {2 * count + 6: 0, 2 * count + 7: 1},
        )(place, window0, *[mine[k] for k in steps], *[other[k] for k in steps], prop,
          *tables, moved, probes)

    before, far, power, window1 = modal_call(
        second_kernel, 3, 4,
        [STRIP, STRIP, MODAL] + TABLES,
        [MODAL, MODAL, PLANE, FIELD],
        (modes, modes, shape(WIN, WIN), shape(2, WIN, WIN)),
        work,
    )(place, row_offset, col_offset, layer1, halo1, moved, *tables)

    power_other = lax.ppermute(power, "zh", [(0, 1), (1, 0)])

    parts_shape = shape(8, 4, 2, 16, WIN)
    piece = shape(2, 2, 32, WIN)
    *pieces, keep, send = modal_call(
        third_kernel, 4, 4,
        [MODAL, MODAL, VMEM, VMEM, MODAL] + [VMEM] * 4 + TABLES,
        [whole(2, 2, 32, WIN)] * 8 + [by_home(), by_home()],
        (piece,) * 8 + (parts_shape, parts_shape),
        [
            pltpu.VMEM((WIN, WIN), F32),
            pltpu.VMEM((2, WIN, WIN), F32),
            pltpu.VMEM((2, WIN, WIN), F32),
            pltpu.VMEM((2, 2, WIN, WIN), F32),
        ],
    )(place, row_offset, col_offset, counts, far, before, window0, window1, probes, prop, power,
      power_other, target, *tables)

    swapped = lax.ppermute(send, "core", [(0, 1), (1, 0)])
    arrived = [pieces[0]]
    for k in range(1, 8):
        arrived.append(lax.ppermute(pieces[k], MODE, ring_route(8, k)))
    kept = keep + swapped
    spread = lax.all_to_all(kept.reshape(32, 2, 16, WIN), SPREAD, 0, 0)
    probe_part = jnp.sum(spread, axis=0)
    own, over = pl.pallas_call(
        gather_kernel,
        out_shape=(shape(2, 2, 32, COLS), shape(2, 2, 32, COLS)),
        in_specs=[SMEM] * 3 + [VMEM] * 8,
        out_specs=[VMEM] * 2,
        compiler_params=PARAMS,
        name="gather",
    )(place, row_offset, col_offset, *arrived)
    over_in = lax.ppermute(over, TILE, ahead)

    total = own + over_in
    parts = []
    for k in range(1, 8):
        parts.append(lax.ppermute(total, MODE, ring_route(8, k)))
    probe_all = lax.all_to_all(jnp.broadcast_to(probe_part, (16, 2, 16, WIN)), TILE, 0, 0)
    object_grad = pl.pallas_call(
        functools.partial(join_kernel, 0, 1),
        out_shape=shape(2, 2, WIN, COLS),
        in_specs=[SMEM, VMEM],
        out_specs=ANY,
        scratch_shapes=[pltpu.SemaphoreType.DMA((8,))],
        compiler_params=PARAMS,
        name="joina",
    )(place, total)
    object_grad = pl.pallas_call(
        functools.partial(join_kernel, 1, 8),
        out_shape=shape(2, 2, WIN, COLS),
        in_specs=[SMEM] + [VMEM] * 7 + [ANY],
        out_specs=ANY,
        scratch_shapes=[pltpu.SemaphoreType.DMA((8,))],
        input_output_aliases={8: 0},
        compiler_params=PARAMS,
        name="joinb",
    )(place, *parts, object_grad)
    probe_grad = jnp.transpose(probe_all, (1, 0, 2, 3)).reshape(1, 2, WIN, WIN)
    return object_grad, probe_grad


def solution(mesh):
    fine = Mesh(mesh.devices.reshape(2, 4, 2, 4, 2), ("zl", "x", "core", "y", "zh"))
    placed = (
        P(None, None, TILE, None),
        P(MODE, None, None, None),
        P(TILE, None, None),
        P(),
        P(TILE),
        P(TILE),
        P(TILE),
    )

    return jax.shard_map(
        per_device,
        mesh=fine,
        in_specs=placed,
        out_specs=(P(None, None, TILE, None), P(MODE, None, None, None)),
        check_vma=False,
    )
```

```python
import functools
import math

import jax
import jax.numpy as jnp
import numpy as np
from jax import lax
from jax.experimental import pallas as pl
from jax.experimental.pallas import tpu as pltpu
from jax.sharding import Mesh, PartitionSpec as P


WIN = 256
HALF = 128
MODES = 8
COLS = 384
F32 = jnp.float32
BF16 = jnp.bfloat16
TILE = ("zl", "x", "core")
MODE = ("y", "zh")
SPREAD = ("zl", "x", "y")
VMEM = pl.BlockSpec(memory_space=pltpu.VMEM)
HBM = pl.BlockSpec(memory_space=pltpu.HBM)
SMEM = pl.BlockSpec(memory_space=pltpu.SMEM)
PARAMS = pltpu.CompilerParams(vmem_limit_bytes=24 * 1024 * 1024)


def make_tables():
    index = np.arange(HALF)
    angle = (index[:, None] * index[None, :] % HALF) * (2.0 * math.pi / HALF)
    cosine, sine = np.cos(angle) / 16.0, np.sin(angle) / 16.0
    ahead = np.block([[cosine, -sine], [sine, cosine]])
    both = []
    for matrix in (ahead, ahead.T):
        high = matrix.astype(np.float32).astype(jnp.bfloat16)
        low = (matrix - high.astype(np.float64)).astype(np.float32).astype(jnp.bfloat16)
        both += [high, low]
    turn = index * (math.pi / HALF)
    lane = np.stack([np.cos(turn), np.sin(turn)])
    lane_table = np.broadcast_to(lane[:, None, :], (2, 8, HALF)).astype(np.float32)
    row_table = np.broadcast_to(lane[:, :, None], (2, HALF, HALF)).astype(np.float32)
    order = np.concatenate([np.arange(0, WIN, 2), np.arange(1, WIN, 2)])
    pick = np.zeros((WIN, WIN), np.float32)
    pick[np.arange(WIN), order] = 1.0
    picks = np.stack([pick, pick.T]).astype(jnp.bfloat16)
    return np.stack(both), lane_table, row_table, picks


def mm(left, right):
    return jnp.dot(left, right, preferred_element_type=F32)


def split(value):
    high = value.astype(BF16)
    return high, (value - high.astype(F32)).astype(BF16)


def dot_right(value, tables, which):
    high, low = split(value)
    return mm(high, tables[which]) + (mm(low, tables[which]) + mm(high, tables[which + 1]))


def dot_left(tables, which, value):
    high, low = split(value)
    return mm(tables[which], high) + (mm(tables[which], low) + mm(tables[which + 1], high))


def right_forward(real, imag, tables, lane):
    rows = real.shape[0]
    cosine, sine = lane[0, 0:1, :], lane[1, 0:1, :]
    ar, br, ai, bi = real[:, :HALF], real[:, HALF:], imag[:, :HALF], imag[:, HALF:]
    dr, di = ar - br, ai - bi
    top = jnp.concatenate([ar + br, ai + bi], axis=1)
    low = jnp.concatenate([dr * cosine + di * sine, di * cosine - dr * sine], axis=1)
    out = dot_right(jnp.concatenate([top, low], axis=0), tables, 0)
    even, odd = out[:rows], out[rows:]
    return (
        jnp.concatenate([even[:, :HALF], odd[:, :HALF]], axis=1),
        jnp.concatenate([even[:, HALF:], odd[:, HALF:]], axis=1),
    )


def right_inverse(real, imag, tables, lane):
    rows = real.shape[0]
    cosine, sine = lane[0, 0:1, :], lane[1, 0:1, :]
    even = jnp.concatenate([real[:, :HALF], imag[:, :HALF]], axis=1)
    odd = jnp.concatenate([real[:, HALF:], imag[:, HALF:]], axis=1)
    out = dot_right(jnp.concatenate([even, odd], axis=0), tables, 2)
    er, ei = out[:rows, :HALF], out[:rows, HALF:]
    pr, pi = out[rows:, :HALF], out[rows:, HALF:]
    tr, ti = pr * cosine - pi * sine, pi * cosine + pr * sine
    return (
        jnp.concatenate([er + tr, er - tr], axis=1),
        jnp.concatenate([ei + ti, ei - ti], axis=1),
    )


def left_forward(real, imag, tables, row):
    width = real.shape[1]
    cosine, sine = row[0], row[1]
    ar, br, ai, bi = real[:HALF], real[HALF:], imag[:HALF], imag[HALF:]
    dr, di = ar - br, ai - bi
    top = jnp.concatenate([ar + br, ai + bi], axis=0)
    low = jnp.concatenate([dr * cosine + di * sine, di * cosine - dr * sine], axis=0)
    out = dot_left(tables, 2, jnp.concatenate([top, low], axis=1))
    even, odd = out[:, :width], out[:, width:]
    return (
        jnp.concatenate([even[:HALF], odd[:HALF]], axis=0),
        jnp.concatenate([even[HALF:], odd[HALF:]], axis=0),
    )


def left_inverse(real, imag, tables, row):
    width = real.shape[1]
    cosine, sine = row[0], row[1]
    even = jnp.concatenate([real[:HALF], imag[:HALF]], axis=0)
    odd = jnp.concatenate([real[HALF:], imag[HALF:]], axis=0)
    out = dot_left(tables, 0, jnp.concatenate([even, odd], axis=1))
    er, ei = out[:HALF, :width], out[HALF:, :width]
    pr, pi = out[:HALF, width:], out[HALF:, width:]
    tr, ti = pr * cosine - pi * sine, pi * cosine + pr * sine
    return (
        jnp.concatenate([er + tr, er - tr], axis=0),
        jnp.concatenate([ei + ti, ei - ti], axis=0),
    )


def times(ar, ai, br, bi):
    return ar * br - ai * bi, ar * bi + ai * br


def times_conj(ar, ai, br, bi):
    return ar * br + ai * bi, ar * bi - ai * br


BLOCKS = (slice(0, HALF), slice(HALF, WIN))


def cut_window(own, halo, row, col, out):
    rows = lax.broadcasted_iota(jnp.int32, (WIN, COLS), 0)
    lanes = lax.broadcasted_iota(jnp.int32, (WIN, HALF), 1)
    for part in range(2):
        chosen = jnp.where(rows < row, halo[part], own[part])
        first = jnp.where(lanes < col, chosen[:, 2 * HALF :], chosen[:, :HALF])
        ring = jnp.concatenate([first, chosen[:, HALF : 2 * HALF]], axis=1)
        ring = pltpu.roll(ring, lax.rem(WIN - row, WIN), 0)
        out[part] = pltpu.roll(ring, lax.rem(WIN - col, WIN), 1)


def reorder(value, picks):
    for side in range(2):
        high, _ = split(value)
        middle, low = split(value - high.astype(F32))
        if side == 0:
            value = mm(picks[0], high) + mm(picks[0], middle) + mm(picks[0], low)
        else:
            value = mm(high, picks[1]) + mm(middle, picks[1]) + mm(low, picks[1])
    return value


def prepare_kernel(phase, picks, out):
    angle = reorder(phase[...], picks)
    out[0] = jnp.cos(angle)
    out[1] = jnp.sin(angle)


def target_kernel(place, measured, picks, out):
    out[...] = reorder(measured[0], picks)


def cut_kernel(place, field, probe, layer0, layer1, half, sem):
    start = pl.multiple_of(place[2] * HALF, HALF)
    copies = (
        pltpu.make_async_copy(field.at[0], layer0, sem.at[0]),
        pltpu.make_async_copy(probe.at[0, :, pl.ds(start, HALF), :], half, sem.at[1]),
        pltpu.make_async_copy(field.at[1], layer1, sem.at[2]),
    )
    for copy in copies:
        copy.start()
    for copy in copies:
        copy.wait()


def spread_modes(pairs, window, prop, tables, lane, row_table, mid, out):
    for rows in BLOCKS:
        for mode, pair in enumerate(pairs):
            real, imag = pair(rows)
            real, imag = times(real, imag, window[0, rows, :], window[1, rows, :])
            real, imag = right_forward(real, imag, tables, lane)
            mid[mode, 0, rows, :] = real
            mid[mode, 1, rows, :] = imag
    for cols in BLOCKS:
        for mode in range(len(pairs)):
            real, imag = left_forward(mid[mode, 0, :, cols], mid[mode, 1, :, cols], tables,
                                      row_table)
            real, imag = times(prop[0, :, cols], prop[1, :, cols], real, imag)
            real, imag = left_inverse(real, imag, tables, row_table)
            out[mode, 0, :, cols] = real
            out[mode, 1, :, cols] = imag


def start_kernel(place, row_off, col_off, own, halo, probe, prop, tables, lane, row_table,
                 moved, probes, window, mid):
    slot = place[0]
    cut_window(own, halo, row_off[slot], col_off[slot], window)
    probes[0] = probe[0]
    spread_modes([lambda rows: (probe[0, 0, rows, :], probe[0, 1, rows, :])], window, prop, tables,
                 lane, row_table, mid, moved)


def first_kernel(count, place, window, *refs):
    mine, other = refs[:count], refs[count : 2 * count]
    prop, tables, lane, row_table, _, _, moved, probes, mid = refs[2 * count :]
    core = place[2]

    def source(mode):
        def pair(rows):
            index = BLOCKS.index(rows)
            values = []
            for part in range(2):
                value = jnp.where(core == index, mine[mode][part], other[mode][part])
                probes[mode, part, rows, :] = value
                values.append(value)
            return values

        return pair

    spread_modes([source(mode) for mode in range(count)], window, prop, tables, lane, row_table,
                 mid, moved)


GROUP = 4


def second_kernel(place, row_off, col_off, own, halo, moved, tables, lane, row_table,
                  before, far, power, window, mid):
    slot = place[0]
    cut_window(own, halo, row_off[slot], col_off[slot], window)
    power[...] = jnp.zeros(power.shape, F32)

    def some_modes(base, carry):
        for rows in BLOCKS:
            for m in range(GROUP):
                mode = GROUP * base + m
                real, imag = right_inverse(
                    moved[mode, 0, rows, :], moved[mode, 1, rows, :], tables, lane
                )
                before[mode, 0, rows, :] = real
                before[mode, 1, rows, :] = imag
                real, imag = times(real, imag, window[0, rows, :], window[1, rows, :])
                real, imag = right_forward(real, imag, tables, lane)
                mid[m, 0, rows, :] = real
                mid[m, 1, rows, :] = imag
        for cols in BLOCKS:
            for m in range(GROUP):
                mode = GROUP * base + m
                real, imag = left_forward(mid[m, 0, :, cols], mid[m, 1, :, cols], tables, row_table)
                far[mode, 0, :, cols] = real
                far[mode, 1, :, cols] = imag
                power[:, cols] += real * real + imag * imag
        return carry

    some_modes(0, 0)


def third_kernel(place, row_off, col_off, counts, far, before, window0, window1, probes, prop,
                 power, power_other, measured, tables, lane, row_table,
                 *rest):
    pieces, (keep, send, weight, mid, late, terms) = rest[:8], rest[8:]
    slot, core = place[0], place[2]
    alive = jnp.where(slot < counts[0], 1.0 / MODES, 0.0).astype(F32)
    weight[...] = (power[...] + power_other[...] - measured[...]) * alive
    terms[...] = jnp.zeros(terms.shape, F32)

    def some_modes(base, carry):
        for cols in BLOCKS:
            scale = weight[:, cols]
            for m in range(GROUP):
                mode = GROUP * base + m
                real, imag = left_inverse(
                    far[mode, 0, :, cols] * scale, far[mode, 1, :, cols] * scale, tables, row_table
                )
                mid[m, 0, :, cols] = real
                mid[m, 1, :, cols] = imag
        for rows in BLOCKS:
            for m in range(GROUP):
                mode = GROUP * base + m
                real, imag = right_inverse(mid[m, 0, rows, :], mid[m, 1, rows, :], tables, lane)
                tr, ti = times_conj(before[mode, 0, rows, :], before[mode, 1, rows, :], real, imag)
                terms[1, 0, rows, :] += tr
                terms[1, 1, rows, :] += ti
                real, imag = times_conj(window1[0, rows, :], window1[1, rows, :], real, imag)
                real, imag = right_forward(real, imag, tables, lane)
                late[m, 0, rows, :] = real
                late[m, 1, rows, :] = imag
        for cols in BLOCKS:
            for m in range(GROUP):
                real, imag = left_forward(late[m, 0, :, cols], late[m, 1, :, cols], tables,
                                          row_table)
                real, imag = times_conj(prop[0, :, cols], prop[1, :, cols], real, imag)
                real, imag = left_inverse(real, imag, tables, row_table)
                mid[m, 0, :, cols] = real
                mid[m, 1, :, cols] = imag
        for index, rows in enumerate(BLOCKS):
            for m in range(GROUP):
                mode = GROUP * base + m
                step = jnp.where(mode < 2, 2 * mode + 1, 2 * mode - 4)
                home = lax.rem(slot - step + 4, 4)
                real, imag = right_inverse(mid[m, 0, rows, :], mid[m, 1, rows, :], tables, lane)
                tr, ti = times_conj(probes[mode, 0, rows, :], probes[mode, 1, rows, :], real, imag)
                terms[0, 0, rows, :] += tr
                terms[0, 1, rows, :] += ti
                pair = times_conj(window0[0, rows, :], window0[1, rows, :], real, imag)
                for part in range(2):
                    for group in range(4):
                        upper = pair[part][group * 32 : group * 32 + 16]
                        lower = pair[part][group * 32 + 16 : group * 32 + 32]
                        keep[index * 4 + group, home, part] = jnp.where(core == 0, upper, lower)
                        send[index * 4 + group, home, part] = jnp.where(core == 0, lower, upper)
        return carry

    some_modes(0, 0)
    for layer in range(2):
        for part in range(2):
            ring = pltpu.roll(terms[layer, part], row_off[slot], 0)
            terms[layer, part] = pltpu.roll(ring, col_off[slot], 1)
    shard = place[0] * 2 + place[1]
    for step in range(8):
        start = pl.multiple_of(lax.rem(shard + step, 8) * 32, 32)
        for layer in range(2):
            for part in range(2):
                pieces[step][layer, part] = terms[layer, part, pl.ds(start, 32), :]


def gather_kernel(place, row_off, col_off, *refs):
    arrived, (own, halo) = refs[:8], refs[8:]
    shard = place[0] * 2 + place[1]
    rows = lax.broadcasted_iota(jnp.int32, (32, HALF), 0) + shard * 32
    lanes = lax.broadcasted_iota(jnp.int32, (32, HALF), 1)
    for layer in range(2):
        for part in range(2):
            mine = [jnp.zeros((32, HALF), F32) for _ in range(3)]
            next_one = [jnp.zeros((32, HALF), F32) for _ in range(3)]
            for step in range(8):
                slot = lax.div(lax.rem(shard - step + 8, 8), 2)
                value = arrived[step][layer, part]
                first, second = value[:, :HALF], value[:, HALF:]
                inside = rows >= row_off[slot]
                turned = lanes < col_off[slot]
                moves = (jnp.where(turned, 0.0, first), second, jnp.where(turned, first, 0.0))
                for place_in, move in enumerate(moves):
                    mine[place_in] = mine[place_in] + jnp.where(inside, move, 0.0)
                    next_one[place_in] = next_one[place_in] + jnp.where(inside, 0.0, move)
            own[layer, part] = jnp.concatenate(mine, axis=1)
            halo[layer, part] = jnp.concatenate(next_one, axis=1)


def total_kernel(spread, out):
    value = jnp.sum(spread[...], axis=0)
    for k in range(16):
        out[k] = value


def join_kernel(place, *refs):
    out, sem = refs[-2], refs[-1]
    shard = place[0] * 2 + place[1]
    copies = []
    for step in range(8):
        start = pl.multiple_of(lax.rem(shard - step + 8, 8) * 32, 32)
        copies.append(
            pltpu.make_async_copy(refs[step], out.at[:, :, pl.ds(start, 32), :], sem.at[step])
        )
    for copy in copies:
        copy.start()
    for copy in copies:
        copy.wait()


def whole(*sizes):
    return pl.BlockSpec(sizes, lambda *_: (0,) * len(sizes))


TABLES = [VMEM, VMEM, VMEM]
PLANE = whole(WIN, WIN)
FIELD = whole(2, WIN, WIN)


ANY = pl.BlockSpec(memory_space=pl.ANY)


def modal_call(body, scalars, steps, ins, outs, out_shape, scratch, aliases=None):
    return pl.pallas_call(
        body,
        out_shape=out_shape,
        grid_spec=pltpu.PrefetchScalarGridSpec(
            num_scalar_prefetch=scalars,
            grid=(steps,),
            in_specs=ins,
            out_specs=outs,
            scratch_shapes=scratch,
        ),
        input_output_aliases=aliases or {},
        compiler_params=PARAMS,
    )


def shape(*sizes):
    return jax.ShapeDtypeStruct(sizes, F32)


def ring_route(size, step):
    return [(i, (i + step) % size) for i in range(size)]


def per_device(object_field, probe, measured, prop_phase, counts, row_offset, col_offset):
    matrices, lane_table, row_table, picks = (jnp.asarray(t) for t in make_tables())
    slot, high, core = lax.axis_index("y"), lax.axis_index("zh"), lax.axis_index("core")
    place = jnp.stack([slot, high, core]).astype(jnp.int32)
    back = [(i, i - 1) for i in range(1, 16)]
    ahead = [(i, i + 1) for i in range(15)]

    layer0, layer1, half = pl.pallas_call(
        cut_kernel,
        out_shape=(shape(2, WIN, COLS), shape(2, WIN, COLS), shape(2, HALF, WIN)),
        in_specs=[SMEM, HBM, HBM],
        out_specs=[VMEM] * 3,
        scratch_shapes=[pltpu.SemaphoreType.DMA((3,))],
        compiler_params=PARAMS,
        name="cut",
    )(place, *(pltpu.with_memory_space_constraint(v, pltpu.HBM) for v in (object_field, probe)))
    halo0 = lax.ppermute(layer0, TILE, back)
    halo1 = lax.ppermute(layer1, TILE, back)
    swap = [(0, 1), (1, 0)]
    mine, other = {}, {}
    for k in (1, 3, 2):
        mine[k] = lax.ppermute(half, "y", ring_route(4, k))
        other[k] = lax.ppermute(mine[k], "core", swap)

    prop = pl.pallas_call(
        prepare_kernel,
        out_shape=shape(2, WIN, WIN),
        in_specs=[VMEM, VMEM],
        out_specs=VMEM,
        compiler_params=PARAMS,
        name="prepare",
    )(prop_phase, picks)
    target = pl.pallas_call(
        target_kernel,
        out_shape=shape(WIN, WIN),
        grid_spec=pltpu.PrefetchScalarGridSpec(
            num_scalar_prefetch=1,
            grid=(1,),
            in_specs=[pl.BlockSpec((1, WIN, WIN), lambda i, p: (p[0], 0, 0)), VMEM],
            out_specs=PLANE,
        ),
        compiler_params=PARAMS,
        name="target",
    )(place, measured, picks)

    modes = shape(4, 2, WIN, WIN)
    tables = (matrices, lane_table, row_table)

    def work(count):
        return [pltpu.VMEM((count, 2, WIN, WIN), F32)]

    def block(size, index):
        return pl.BlockSpec((size, 2, WIN, WIN), lambda *_: (index, 0, 0, 0))

    moved, probes, window0 = modal_call(
        start_kernel, 3, 1,
        [VMEM] * 4 + TABLES,
        [block(1, 2), block(1, 2), FIELD], (modes, modes, shape(2, WIN, WIN)), work(1),
    )(place, row_offset, col_offset, layer0, halo0, probe, prop, *tables)
    for steps, index in (((1, 3), 0), ((2,), 3)):
        count = len(steps)
        moved, probes = modal_call(
            functools.partial(first_kernel, count), 1, 1,
            [VMEM] * (2 * count + 2) + TABLES + [ANY, ANY],
            [block(count, index)] * 2, (modes, modes), work(count),
            {2 * count + 6: 0, 2 * count + 7: 1},
        )(place, window0, *[mine[k] for k in steps], *[other[k] for k in steps], prop,
          *tables, moved, probes)

    before, far, power, window1 = pl.pallas_call(
        second_kernel,
        in_specs=[SMEM] * 3 + [VMEM] * 6,
        out_specs=[VMEM] * 4,
        out_shape=(modes, modes, shape(WIN, WIN), shape(2, WIN, WIN)),
        scratch_shapes=work(GROUP),
        compiler_params=PARAMS,
        name="second",
    )(place, row_offset, col_offset, layer1, halo1, moved, *tables)

    power_other = lax.ppermute(power, "zh", [(0, 1), (1, 0)])

    parts_shape = shape(8, 4, 2, 16, WIN)
    piece = shape(2, 2, 32, WIN)
    *pieces, keep, send = pl.pallas_call(
        third_kernel,
        in_specs=[SMEM] * 4 + [VMEM] * 12,
        out_specs=[VMEM] * 10,
        out_shape=(piece,) * 8 + (parts_shape, parts_shape),
        scratch_shapes=[pltpu.VMEM((WIN, WIN), F32)] + work(GROUP) * 3,
        compiler_params=PARAMS,
        name="third",
    )(place, row_offset, col_offset, counts, far, before, window0, window1, probes, prop, power,
      power_other, target, *tables)

    swapped = lax.ppermute(send, "core", [(0, 1), (1, 0)])
    arrived = [pieces[0]]
    for k in range(1, 8):
        arrived.append(lax.ppermute(pieces[k], MODE, ring_route(8, k)))
    kept = keep + swapped
    spread = lax.all_to_all(kept.reshape(32, 2, 16, WIN), SPREAD, 0, 0)
    own, over = pl.pallas_call(
        gather_kernel,
        out_shape=(shape(2, 2, 32, COLS), shape(2, 2, 32, COLS)),
        in_specs=[SMEM] * 3 + [VMEM] * 8,
        out_specs=[VMEM] * 2,
        compiler_params=PARAMS,
        name="gather",
    )(place, row_offset, col_offset, *arrived)
    over_in = lax.ppermute(over, TILE, ahead)

    total = own + over_in
    parts = [total]
    for k in range(1, 8):
        parts.append(lax.ppermute(total, MODE, ring_route(8, k)))
    probe_part = pl.pallas_call(
        total_kernel,
        in_specs=[VMEM],
        out_specs=VMEM,
        out_shape=shape(16, 2, 16, WIN),
        compiler_params=PARAMS,
        name="psum",
    )(spread)
    probe_all = lax.all_to_all(probe_part, TILE, 0, 0)
    object_grad = pl.pallas_call(
        join_kernel,
        out_shape=shape(2, 2, WIN, COLS),
        in_specs=[SMEM] + [VMEM] * 8,
        out_specs=ANY,
        scratch_shapes=[pltpu.SemaphoreType.DMA((8,))],
        compiler_params=PARAMS,
        name="join",
    )(place, *parts)
    probe_grad = jnp.transpose(probe_all, (1, 0, 2, 3)).reshape(1, 2, WIN, WIN)
    return object_grad, probe_grad


def solution(mesh):
    fine = Mesh(mesh.devices.reshape(2, 4, 2, 4, 2), ("zl", "x", "core", "y", "zh"))
    placed = (
        P(None, None, TILE, None),
        P(MODE, None, None, None),
        P(TILE, None, None),
        P(),
        P(TILE),
        P(TILE),
        P(TILE),
    )

    return jax.shard_map(
        per_device,
        mesh=fine,
        in_specs=placed,
        out_specs=(P(None, None, TILE, None), P(MODE, None, None, None)),
        check_vma=False,
    )
```
